256 devices in a mesh: sample: 16 (over y_hi, z), variant: 16 (over y_lo, x, core).
Axes of the slice: x: 4, y: 4 (y_hi: 2, y_lo: 2; y = y_hi * 2 + y_lo), z: 8, core: 2. Of those that a mesh axis runs over, the one named last changes fastest.
Arguments:
- dosage: bfloat16 [8192, 8192], P('sample', 'variant'), may hold values from 0 to 2
- covariates: float32 [30, 8192], P(None, 'sample'), may hold values from -6 to 6
- reach: int32 [16], replicated, may hold values from 1 to 2, as said below
Outputs:
- ld_bands: bfloat16 [4, 8192, 512], P(None, ('variant', 'sample'))
The draws below stay inside these ranges and needn't reach their ends.
Inputs may be any that keep to these rules, and one draw needn't show every extreme that they name: `reach`: every draw has a block whose band reaches 2 blocks on each side.
All inputs are finite; a program needn't handle non-finite values.
Results may differ from the reference program's by a relative error of at most 0.015.
Values may be sent and summed in bfloat16 or wider, within the bound.
No kernel may reach another device: no remote copies, remote signals or barrier semaphores. Data moves between devices by JAX's collectives and lax.ppermute only.
A program may use at most 64 MiB of HBM per device.

```python
import math
import jax
import jax.numpy as jnp
from jax import lax

VB = 512
K = 30
MAXR = 2
S = 8192
NB = 16
V = 8192


def shared_covariates(key):
    values = jax.random.normal(jax.random.fold_in(key, 11), (K, S), jnp.float32)
    return jnp.clip(values, -6.0, 6.0)


def draw_covariates(key, part):
    return shared_covariates(key)


def draw_dosage(key, part):
    values = shared_covariates(key)
    loading = jax.random.normal(jax.random.fold_in(key, 13), (K, V), jnp.float32) / jnp.sqrt(float(K))
    noise = jax.random.uniform(jax.random.fold_in(key, 14), (S, V), jnp.float32, -1.0, 1.0)
    linked = jnp.dot(values.T, loading)
    return jnp.clip(1.0 + 0.3 * linked + 0.45 * noise, 0.0, 2.0).astype(jnp.bfloat16)


def draw_reach(key, part):
    base = jax.random.randint(jax.random.fold_in(key, 21), (NB,), 1, MAXR + 1)
    chosen = jax.random.randint(jax.random.fold_in(key, 22), (), 0, NB)
    return jnp.where(jnp.arange(NB) == chosen, MAXR, base).astype(jnp.int32)


def setup_inputs(seed: int = 0) -> dict:
    streams_of = jax.random.split(jax.random.key(seed), 4)
    return {
        "dosage": draw_dosage(jax.random.fold_in(streams_of[3], 71), 0),
        "covariates": draw_covariates(jax.random.fold_in(streams_of[3], 71), 0),
        "reach": draw_reach(jax.random.fold_in(streams_of[3], 71), 0),
    }


def reference(dosage, covariates, reach):
    highest = lax.Precision.HIGHEST
    samples = dosage.shape[0]
    blocks_count = reach.shape[0]
    design = jnp.concatenate([jnp.ones((1, samples), jnp.float32), covariates.astype(jnp.float32)], 0)
    genotype = dosage.astype(jnp.float32)
    moment = jnp.dot(design, design.T, precision=highest)
    cross = jnp.dot(design, genotype, precision=highest)
    factor = jnp.linalg.cholesky(moment)
    coefficients = jax.scipy.linalg.cho_solve((factor, True), cross)
    residual = genotype - jnp.dot(design.T, coefficients, precision=highest)
    spread = lax.optimization_barrier(jnp.sum(residual * residual, 0))
    scaled = (residual * jnp.sqrt(samples / spread)).astype(jnp.bfloat16)
    stacked = scaled.reshape(samples, blocks_count, VB).transpose(1, 0, 2)
    inverse_root = 1.0 / math.sqrt(samples)

    def one_block(index):
        left = stacked[index].astype(jnp.float32)
        tiles = []
        for slot in range(2 * MAXR):
            offset = slot - MAXR if slot < MAXR else slot - MAXR + 1
            other = ((index + offset) % blocks_count).astype(jnp.int32)
            right = stacked[other].astype(jnp.float32)
            tile = lax.dot_general(left, right, (((0,), (0,)), ((), ())), precision=highest) * inverse_root
            live = abs(offset) <= reach[index]
            tiles.append(jnp.where(live, tile, 0.0).astype(jnp.bfloat16))
        return jnp.stack(tiles)
    result = lax.map(one_block, jnp.arange(blocks_count, dtype=jnp.int32))
    return result.transpose(1, 0, 2, 3).reshape(2 * MAXR, blocks_count * VB, VB)
```

```python
import math

import jax
import jax.numpy as jnp
from jax import lax
from jax.sharding import PartitionSpec as P

MAXR = 2
HIGHEST = lax.Precision.HIGHEST


def exchange(x):
    return lax.all_to_all(x, "sample", 0, 0, tiled=False)


def neighbours(block, core):
    count = lax.axis_size("variant")
    devices = range(count)
    up = lax.ppermute(block, "variant", [((i + 2) % count, i) for i in devices])
    down = lax.ppermute(block, "variant", [((i - 2) % count, i) for i in devices])
    swap = [(i, i ^ 1) for i in devices]
    mate = lax.ppermute(block, "variant", swap)
    other = lax.ppermute(jnp.where(core == 0, up, down), "variant", swap)
    after = jnp.where(core == 0, mate, other)
    before = jnp.where(core == 0, other, mate)
    return [down, before, after, up]


def shards(dosage, covariates, reach):
    local_samples, width = dosage.shape
    parts = lax.axis_size("sample")
    samples = local_samples * parts
    core = lax.axis_index("variant") % 2
    rows = covariates.shape[0] + 1
    padded = -(-rows // parts) * parts
    blank = jnp.zeros((padded - rows, local_samples), jnp.float32)
    design = jnp.concatenate([jnp.ones((1, local_samples), jnp.float32), covariates, blank], 0)

    def sums(block):
        return jnp.dot(design, block.astype(jnp.float32), precision=HIGHEST)

    moment_local = jnp.dot(design, design.T, precision=HIGHEST)
    local = jnp.concatenate([sums(dosage), moment_local], 1)
    around = neighbours(dosage, core)
    chunk = exchange(local.reshape(parts, padded // parts, -1)).sum(0)
    total = exchange(jnp.broadcast_to(chunk[None], (parts,) + chunk.shape)).reshape(padded, -1)
    cross = total[:, :width]
    moment = total[:rows, width : width + rows]
    crosses = neighbours(cross, core)
    factor = jnp.linalg.cholesky(moment)
    inverse = jax.scipy.linalg.solve_triangular(factor, jnp.eye(rows, dtype=jnp.float32), lower=True)

    def residual(block, cross):
        half = jnp.dot(inverse, cross[:rows], precision=HIGHEST)
        coefficients = jnp.dot(inverse.T, half, precision=HIGHEST)
        left = block.astype(jnp.float32) - jnp.dot(design[:rows].T, coefficients, precision=HIGHEST)
        spread = jnp.sum(left * left, 0)
        high = spread.astype(jnp.bfloat16)
        low = (spread - high.astype(jnp.float32)).astype(jnp.bfloat16)
        return left.astype(jnp.bfloat16), jnp.stack([high, low])

    own, own_spread = residual(dosage, cross)
    tiles, spreads = [], [own_spread]
    for block, cross in zip(around, crosses):
        other, spread = residual(block, cross)
        spreads.append(spread)
        tile = lax.dot_general(own, other, (((0,), (0,)), ((), ())), preferred_element_type=jnp.float32)
        tiles.append(tile.astype(jnp.bfloat16).reshape(parts, width // parts, width))
    spreads = jnp.concatenate(spreads, 0)
    spreads = jnp.pad(spreads, ((0, 6), (0, 0)))
    message = jnp.concatenate(tiles + [jnp.broadcast_to(spreads[None], (parts,) + spreads.shape)], 1)
    arrived = exchange(message)
    whole = arrived.astype(jnp.float32).sum(0)
    share = width // parts
    bands = whole[: 2 * MAXR * share].reshape(2 * MAXR, share, width)
    spread = whole[2 * MAXR * share :]
    spread = spread[0:10:2] + spread[1:10:2]
    weight = jnp.sqrt(samples / spread)
    own_weight = lax.dynamic_slice(weight[0], (lax.axis_index("sample") * share,), (share,))
    own_reach = reach[lax.axis_index("variant")]
    offsets = jnp.array([2, 1, 1, 2], jnp.int32)
    scaled = bands * own_weight[None, :, None] * weight[1:][:, None, :] * (1.0 / math.sqrt(samples))
    return jnp.where((offsets <= own_reach)[:, None, None], scaled, 0.0).astype(jnp.bfloat16)


def solution(mesh):
    placed = (P("sample", "variant"), P(None, "sample"), P())
    return jax.shard_map(
        shards,
        mesh=mesh,
        in_specs=placed,
        out_specs=P(None, ("variant", "sample"), None),
        check_vma=False,
    )
```

```python
import math

import jax
import jax.numpy as jnp
from jax import lax
from jax.experimental import pallas as pl
from jax.experimental.pallas import tpu as pltpu
from jax.sharding import PartitionSpec as P

MAXR = 2
HIGHEST = lax.Precision.HIGHEST
BF16 = jnp.bfloat16
F32 = jnp.float32
LANES = 128
STEP = 128
COLUMNS_TOGETHER = (((0,), (0,)), ((), ()))


def split(value):
    high = value.astype(BF16)
    rest = value - high.astype(F32)
    middle = rest.astype(BF16)
    low = (rest - middle.astype(F32)).astype(BF16)
    return high, middle, low


def fill_design(design_ref, covariates_ref):
    count = covariates_ref.shape[0]
    design_ref[...] = jnp.zeros_like(design_ref)
    design_ref[:count, :] = covariates_ref[...]
    design_ref[count : count + 1, :] = jnp.ones((1, design_ref.shape[1]), F32)


def sums_kernel(dosage_ref, covariates_ref, out_ref, design_ref):
    fill_design(design_ref, covariates_ref)
    width = dosage_ref.shape[1]
    padded = design_ref.shape[0]
    design = design_ref[...]
    stacked = jnp.concatenate(split(design), 0)
    parts = jnp.dot(stacked, dosage_ref[...], preferred_element_type=F32)
    out_ref[:, :width] = parts[:padded] + parts[padded : 2 * padded] + parts[2 * padded :]
    moment = lax.dot_general(
        design, design, (((1,), (1,)), ((), ())), precision=HIGHEST, preferred_element_type=F32
    )
    out_ref[:, width:] = jnp.concatenate(
        [moment, jnp.zeros((padded, out_ref.shape[1] - width - padded), F32)], 1
    )


def local_sums(dosage, covariates, padded):
    samples, width = dosage.shape
    return pl.pallas_call(
        sums_kernel,
        out_shape=jax.ShapeDtypeStruct((padded, width + LANES), F32),
        scratch_shapes=[pltpu.VMEM((padded, samples), F32)],
        name="local_sums",
    )(dosage, covariates)


def tiles_kernel(
    own0, own1, far0, far1, near0, near1, cov0, cov1, cross_own, cross_far, cross_near, inverse,
    out_ref, design, left, right,
):
    samples, width = own0.shape
    parts = out_ref.shape[0]
    share = width // parts
    fill_design(design.at[:, :samples], cov0)
    fill_design(design.at[:, samples:], cov1)
    factor = inverse[...]
    h, m, l = split(jnp.dot(factor, design[...], precision=HIGHEST, preferred_element_type=F32))
    white = jnp.concatenate([h, h, m, h, l, m], 0)

    def residual(pieces, cross, target):
        h, m, l = split(jnp.dot(factor, cross[...], precision=HIGHEST, preferred_element_type=F32))
        stacked = jnp.concatenate([h, m, h, l, h, m], 0)
        spread = jnp.zeros((1, width), F32)
        for index, piece in enumerate(pieces):
            for start in range(0, samples, STEP):
                at = index * samples + start
                fitted = lax.dot_general(
                    white[:, at : at + STEP], stacked, COLUMNS_TOGETHER, preferred_element_type=F32
                )
                rest = piece[start : start + STEP, :].astype(F32) - fitted
                spread = spread + jnp.sum(rest * rest, 0, keepdims=True)
                target[at : at + STEP, :] = rest.astype(BF16)
        high = spread.astype(BF16)
        low = (spread - high.astype(F32)).astype(BF16)
        return [high, low]

    rows = residual((own0, own1), cross_own, left)
    for slot, (pieces, cross) in enumerate((((far0, far1), cross_far), ((near0, near1), cross_near))):
        rows += residual(pieces, cross, right)
        tile = lax.dot_general(left[...], right[...], COLUMNS_TOGETHER, preferred_element_type=F32)
        tile = tile.astype(BF16)
        for part in range(parts):
            out_ref[part, slot * share : (slot + 1) * share, :] = tile[part * share : (part + 1) * share]
    rows.append(jnp.zeros((8 - len(rows), width), BF16))
    rows = jnp.concatenate(rows, 0)
    for part in range(parts):
        out_ref[part, 2 * share :, :] = rows


def tiles(pieces, designs, crosses, inverse, parts):
    samples, width = pieces[0].shape
    padded = inverse.shape[0]
    return pl.pallas_call(
        tiles_kernel,
        out_shape=jax.ShapeDtypeStruct((parts, 2 * (width // parts) + 8, width), BF16),
        scratch_shapes=[
            pltpu.VMEM((padded, 2 * samples), F32),
            pltpu.VMEM((2 * samples, width), BF16),
            pltpu.VMEM((2 * samples, width), BF16),
        ],
        compiler_params=pltpu.CompilerParams(vmem_limit_bytes=40 << 20),
        name="tiles",
    )(*pieces, *designs, *crosses, inverse)


def exchange(x):
    return lax.all_to_all(x, "sample", 0, 0, tiled=False)


def shards(dosage, covariates, reach):
    local_samples, width = dosage.shape
    parts = lax.axis_size("sample")
    blocks = lax.axis_size("variant")
    half = parts // 2
    samples = local_samples * parts
    place = lax.axis_index("sample")
    core = lax.axis_index("variant") % 2
    side = place // half
    rows = covariates.shape[0] + 1
    padded = -(-rows // parts) * parts
    both = ("sample", "variant")

    partner_route = [(i, i ^ half) for i in range(parts)]
    core_route = [(i, i ^ 1) for i in range(blocks)]
    far_route = []
    for s in range(parts):
        step = MAXR if s < half else -MAXR
        for v in range(blocks):
            far_route.append((s * blocks + (v + step) % blocks, s * blocks + v))

    def from_partner(x):
        return lax.ppermute(x, "sample", partner_route)

    def from_far(x):
        return lax.ppermute(x, both, far_route)

    def from_near(own, far):
        return lax.ppermute(jnp.where(core != side, own, far), "variant", core_route)

    own0 = dosage
    far0 = from_far(own0)
    own1 = from_partner(own0)
    covariates1 = from_partner(covariates)
    local = local_sums(dosage, covariates, padded)
    chunk = exchange(local.reshape(parts, padded // parts, -1)).sum(0)
    far1 = from_far(own1)
    near0 = from_near(own0, far0)
    total = exchange(jnp.broadcast_to(chunk[None], (parts,) + chunk.shape)).reshape(padded, -1)
    near1 = from_near(own1, far1)
    cross = total[:, :width]
    cross_far = from_far(cross)
    cross_near = from_near(cross, cross_far)
    moment = total[:rows, width : width + rows]
    factor = jnp.linalg.cholesky(moment)
    inverse = jax.scipy.linalg.solve_triangular(factor, jnp.eye(rows, dtype=F32), lower=True)
    inverse = jnp.pad(inverse, ((0, padded - rows), (0, padded - rows)))
    message = tiles(
        (own0, own1, far0, far1, near0, near1),
        (covariates, covariates1),
        (cross, cross_far, cross_near),
        inverse,
        parts,
    )
    share = width // parts
    arrived = exchange(message).reshape(2, half, 2 * share + 8, width)
    whole = arrived.astype(F32).sum(1)
    far, near = whole[:, :share], whole[:, share : 2 * share]
    bands = jnp.stack([far[1], near[1], near[0], far[0]])
    spread = whole[:, 2 * share : 2 * share + 6 : 2] + whole[:, 2 * share + 1 : 2 * share + 6 : 2]
    weight = jnp.sqrt(samples / spread)
    columns = jnp.stack([weight[1, 1], weight[1, 2], weight[0, 2], weight[0, 1]])
    own_weight = lax.dynamic_slice(weight[0, 0], (place * share,), (share,))
    own_reach = reach[lax.axis_index("variant")]
    offsets = jnp.array([2, 1, 1, 2], jnp.int32)
    scaled = bands * own_weight[None, :, None] * columns[:, None, :] * (1.0 / math.sqrt(samples))
    return jnp.where((offsets <= own_reach)[:, None, None], scaled, 0.0).astype(BF16)


def solution(mesh):
    placed = (P("sample", "variant"), P(None, "sample"), P())
    return jax.shard_map(
        shards,
        mesh=mesh,
        in_specs=placed,
        out_specs=P(None, ("variant", "sample"), None),
        check_vma=False,
    )
```

```python
import math

import jax
import jax.numpy as jnp
from jax import lax
from jax.experimental import pallas as pl
from jax.experimental.pallas import tpu as pltpu
from jax.sharding import PartitionSpec as P

MAXR = 2
HIGHEST = lax.Precision.HIGHEST
BF16 = jnp.bfloat16
F32 = jnp.float32
LANES = 128
STEP = 128
COLUMNS_TOGETHER = (((0,), (0,)), ((), ()))


def split(value):
    high = value.astype(BF16)
    rest = value - high.astype(F32)
    middle = rest.astype(BF16)
    low = (rest - middle.astype(F32)).astype(BF16)
    return high, middle, low


def fill_design(design_ref, covariates_ref):
    count = covariates_ref.shape[0]
    design_ref[...] = jnp.zeros_like(design_ref)
    design_ref[:count, :] = covariates_ref[...]
    design_ref[count : count + 1, :] = jnp.ones((1, design_ref.shape[1]), F32)


def sums_kernel(dosage_ref, covariates_ref, out_ref, design_ref):
    fill_design(design_ref, covariates_ref)
    width = dosage_ref.shape[1]
    padded = design_ref.shape[0]
    design = design_ref[...]
    stacked = jnp.concatenate(split(design), 0)
    parts = jnp.dot(stacked, dosage_ref[...], preferred_element_type=F32)
    out_ref[:, :width] = parts[:padded] + parts[padded : 2 * padded] + parts[2 * padded :]
    moment = lax.dot_general(
        design, design, (((1,), (1,)), ((), ())), precision=HIGHEST, preferred_element_type=F32
    )
    out_ref[:, width:] = jnp.concatenate(
        [moment, jnp.zeros((padded, out_ref.shape[1] - width - padded), F32)], 1
    )


def local_sums(dosage, covariates, padded):
    samples, width = dosage.shape
    return pl.pallas_call(
        sums_kernel,
        out_shape=jax.ShapeDtypeStruct((padded, width + LANES), F32),
        scratch_shapes=[pltpu.VMEM((padded, samples), F32)],
        name="local_sums",
    )(dosage, covariates)


def tiles_kernel(
    own0, own1, far0, far1, near0, near1, cov0, cov1, cross_own, cross_far, cross_near, inverse,
    out_ref, design, left, right,
):
    samples, width = own0.shape
    parts = out_ref.shape[0]
    share = width // parts
    fill_design(design.at[:, :samples], cov0)
    fill_design(design.at[:, samples:], cov1)
    factor = inverse[...]
    h, m, l = split(jnp.dot(factor, design[...], precision=HIGHEST, preferred_element_type=F32))
    white = jnp.concatenate([h, h, m, h, l, m], 0)

    def residual(pieces, cross, target):
        h, m, l = split(jnp.dot(factor, cross[...], precision=HIGHEST, preferred_element_type=F32))
        stacked = jnp.concatenate([h, m, h, l, h, m], 0)
        spread = jnp.zeros((1, width), F32)
        for index, piece in enumerate(pieces):
            for start in range(0, samples, STEP):
                at = index * samples + start
                fitted = lax.dot_general(
                    white[:, at : at + STEP], stacked, COLUMNS_TOGETHER, preferred_element_type=F32
                )
                rest = piece[start : start + STEP, :].astype(F32) - fitted
                spread = spread + jnp.sum(rest * rest, 0, keepdims=True)
                target[at : at + STEP, :] = rest.astype(BF16)
        high = spread.astype(BF16)
        low = (spread - high.astype(F32)).astype(BF16)
        return [high, low]

    rows = residual((own0, own1), cross_own, left)
    for slot, (pieces, cross) in enumerate((((far0, far1), cross_far), ((near0, near1), cross_near))):
        rows += residual(pieces, cross, right)
        tile = lax.dot_general(left[...], right[...], COLUMNS_TOGETHER, preferred_element_type=F32)
        tile = tile.astype(BF16)
        for part in range(parts):
            out_ref[part, slot * share : (slot + 1) * share, :] = tile[part * share : (part + 1) * share]
    rows.append(jnp.zeros((8 - len(rows), width), BF16))
    rows = jnp.concatenate(rows, 0)
    for part in range(parts):
        out_ref[part, 2 * share :, :] = rows


def tiles(pieces, designs, crosses, inverse, parts):
    samples, width = pieces[0].shape
    padded = inverse.shape[0]
    return pl.pallas_call(
        tiles_kernel,
        out_shape=jax.ShapeDtypeStruct((parts, 2 * (width // parts) + 8, width), BF16),
        scratch_shapes=[
            pltpu.VMEM((padded, 2 * samples), F32),
            pltpu.VMEM((2 * samples, width), BF16),
            pltpu.VMEM((2 * samples, width), BF16),
        ],
        compiler_params=pltpu.CompilerParams(vmem_limit_bytes=40 << 20),
        name="tiles",
    )(*pieces, *designs, *crosses, inverse)


def exchange(x):
    return lax.all_to_all(x, "sample", 0, 0, tiled=False)


def shards(dosage, covariates, reach):
    local_samples, width = dosage.shape
    parts = lax.axis_size("sample")
    blocks = lax.axis_size("variant")
    half = parts // 2
    samples = local_samples * parts
    place = lax.axis_index("sample")
    core = lax.axis_index("variant") % 2
    side = place % 2
    rows = covariates.shape[0] + 1
    padded = -(-rows // parts) * parts
    both = ("sample", "variant")

    partner_route = [(i, i ^ 1) for i in range(parts)]
    core_route = [(i, i ^ 1) for i in range(blocks)]
    far_route = []
    for s in range(parts):
        step = MAXR if s % 2 == 0 else -MAXR
        for v in range(blocks):
            far_route.append((s * blocks + (v + step) % blocks, s * blocks + v))

    def from_partner(x):
        return lax.ppermute(x, "sample", partner_route)

    def from_far(x):
        return lax.ppermute(x, both, far_route)

    def for_mate(own, far):
        return jnp.where(core != side, own, far)

    def swap(x):
        return lax.ppermute(x, "variant", core_route)

    def after(x, *earlier):
        return lax.optimization_barrier((x,) + earlier)[0]

    own0 = dosage
    covariates1 = from_partner(covariates)
    message = local_sums(dosage, covariates, padded).reshape(parts, padded // parts, -1)
    sent = own0
    own1 = from_partner(sent)
    far0 = from_far(sent)
    chunk = exchange(message).sum(0)
    message = jnp.broadcast_to(chunk[None], (parts,) + chunk.shape)
    far1 = from_far(after(own1, message))
    message = after(message, own1, far0)
    total = exchange(message).reshape(padded, -1)
    give0, give1 = for_mate(own0, far0), for_mate(own1, far1)
    near0, near1 = swap(give0), swap(give1)
    cross = total[:, :width]
    cross_far = from_far(cross)
    cross_near = swap(for_mate(cross, cross_far))
    moment = total[:rows, width : width + rows]
    factor = jnp.linalg.cholesky(moment)
    inverse = jax.scipy.linalg.solve_triangular(factor, jnp.eye(rows, dtype=F32), lower=True)
    inverse = jnp.pad(inverse, ((0, padded - rows), (0, padded - rows)))
    message = tiles(
        (own0, own1, far0, far1, near0, near1),
        (covariates, covariates1),
        (cross, cross_far, cross_near),
        inverse,
        parts,
    )
    share = width // parts
    arrived = exchange(message).reshape(half, 2, 2 * share + 8, width)
    whole = arrived.astype(F32).sum(0)
    far, near = whole[:, :share], whole[:, share : 2 * share]
    bands = jnp.stack([far[1], near[1], near[0], far[0]])
    spread = whole[:, 2 * share : 2 * share + 6 : 2] + whole[:, 2 * share + 1 : 2 * share + 6 : 2]
    weight = jnp.sqrt(samples / spread)
    columns = jnp.stack([weight[1, 1], weight[1, 2], weight[0, 2], weight[0, 1]])
    own_weight = lax.dynamic_slice(weight[0, 0], (place * share,), (share,))
    own_reach = reach[lax.axis_index("variant")]
    offsets = jnp.array([2, 1, 1, 2], jnp.int32)
    scaled = bands * own_weight[None, :, None] * columns[:, None, :] * (1.0 / math.sqrt(samples))
    return jnp.where((offsets <= own_reach)[:, None, None], scaled, 0.0).astype(BF16)


def solution(mesh):
    placed = (P("sample", "variant"), P(None, "sample"), P())
    return jax.shard_map(
        shards,
        mesh=mesh,
        in_specs=placed,
        out_specs=P(None, ("variant", "sample"), None),
        check_vma=False,
    )
```

```python
import functools
import math

import jax
import jax.numpy as jnp
from jax import lax
from jax.experimental import pallas as pl
from jax.experimental.pallas import tpu as pltpu
from jax.sharding import PartitionSpec as P

MAXR = 2
HIGHEST = lax.Precision.HIGHEST
BF16 = jnp.bfloat16
F32 = jnp.float32
LANES = 128
STEP = 128
COLUMNS_TOGETHER = (((0,), (0,)), ((), ()))


def split(value):
    high = value.astype(BF16)
    rest = value - high.astype(F32)
    middle = rest.astype(BF16)
    low = (rest - middle.astype(F32)).astype(BF16)
    return high, middle, low


def fill_design(design_ref, covariates_ref):
    count = covariates_ref.shape[0]
    design_ref[...] = jnp.zeros_like(design_ref)
    design_ref[:count, :] = covariates_ref[...]
    design_ref[count : count + 1, :] = jnp.ones((1, design_ref.shape[1]), F32)


def sums_kernel(dosage_ref, covariates_ref, out_ref, design_ref):
    fill_design(design_ref, covariates_ref)
    width = dosage_ref.shape[1]
    padded = design_ref.shape[0]
    design = design_ref[...]
    stacked = jnp.concatenate(split(design), 0)
    parts = jnp.dot(stacked, dosage_ref[...], preferred_element_type=F32)
    cross = parts[:padded] + parts[padded : 2 * padded] + parts[2 * padded :]
    moment = lax.dot_general(
        design, design, (((1,), (1,)), ((), ())), precision=HIGHEST, preferred_element_type=F32
    )
    left = jnp.zeros((padded, LANES // 2), F32)
    right = jnp.zeros((padded, LANES - LANES // 2 - padded), F32)
    moment = jnp.concatenate([left, moment, right], 1)
    each = out_ref.shape[1]
    for part in range(out_ref.shape[0]):
        out_ref[part, :, :width] = cross[part * each : (part + 1) * each]
        out_ref[part, :, width:] = moment[part * each : (part + 1) * each]


def local_sums(dosage, covariates, padded, parts):
    samples, width = dosage.shape
    return pl.pallas_call(
        sums_kernel,
        out_shape=jax.ShapeDtypeStruct((parts, padded // parts, width + LANES), F32),
        scratch_shapes=[pltpu.VMEM((padded, samples), F32)],
        name="local_sums",
    )(dosage, covariates)


def factor(total, count):
    padded, width = total.shape[0], total.shape[1] - LANES
    row = lax.broadcasted_iota(jnp.int32, (padded, LANES), 0)
    lane = lax.broadcasted_iota(jnp.int32, (padded, LANES), 1)
    first = LANES // 2
    spare = (row >= count) & (lane == row + first)
    work = total[:, width:] + jnp.where((lane == row) | spare, 1.0, 0.0)
    for step in range(count - 1):
        pivot_row = work[step : step + 1, :]
        pivot_row = pivot_row / pivot_row[:, first + step : first + step + 1]
        column = jnp.broadcast_to(work[:, first + step : first + step + 1], work.shape)
        work = work - jnp.where(row > step, column, 0.0) * pivot_row
    diagonal = jnp.sum(jnp.where(lane == row + first, work, 0.0), 1, keepdims=True)
    return work[:, :padded], work[:, :padded] / diagonal


def residual(pieces, cross, solved, white, target):
    h, m, l = split(jnp.dot(solved, cross, precision=HIGHEST, preferred_element_type=F32))
    stacked = jnp.concatenate([h, m, h, l, h, m], 0)
    spread = jnp.zeros((1, stacked.shape[1]), F32)
    at = 0
    for piece in pieces:
        for start in range(0, piece.shape[0], STEP):
            fitted = lax.dot_general(
                white[:, at : at + STEP], stacked, COLUMNS_TOGETHER, preferred_element_type=F32
            )
            rest = piece[start : start + STEP, :].astype(F32) - fitted
            spread = spread + jnp.sum(rest * rest, 0, keepdims=True)
            target[at : at + STEP, :] = rest.astype(BF16)
            at += STEP
    high = spread.astype(BF16)
    low = (spread - high.astype(F32)).astype(BF16)
    return [high, low]


def tile_of(left, right):
    tile = lax.dot_general(left[...], right[...], COLUMNS_TOGETHER, preferred_element_type=F32)
    return tile.astype(BF16)


def own_kernel(count, own0, own1, cov0, cov1, total, solved_ref, white_ref, left, rows_ref, design):
    samples, width = own0.shape
    fill_design(design.at[:, :samples], cov0)
    fill_design(design.at[:, samples:], cov1)
    unit, solved = factor(total[...], count)
    h, m, l = split(jnp.dot(unit, design[...], precision=HIGHEST, preferred_element_type=F32))
    white = jnp.concatenate([h, h, m, h, l, m], 0)
    white_ref[...] = white
    solved_ref[...] = solved
    rows = residual((own0, own1), total[:, :width], solved, white, left)
    rows_ref[...] = jnp.concatenate(rows, 0)


def far_kernel(far0, far1, cross_far, solved, white, left, own_rows, tile_ref, rows_ref, right):
    rows = residual((far0, far1), cross_far[...], solved[...], white[...], right)
    tile_ref[...] = tile_of(left, right)
    rows_ref[...] = jnp.concatenate([own_rows[...]] + rows, 0)


def near_kernel(
    near0, near1, cross_near, solved, far_tile_ref, left, white, rows_ref, out_ref, right
):
    width = near0.shape[1]
    share = width // out_ref.shape[0]
    rows = [rows_ref[...]] + residual((near0, near1), cross_near[...], solved[...], white[...], right)
    tile = tile_of(left, right)
    extra = out_ref.shape[1] - 2 * share
    rows = jnp.concatenate(rows + [jnp.zeros((extra - 6, width), BF16)], 0)
    for part in range(out_ref.shape[0]):
        at = slice(part * share, (part + 1) * share)
        out_ref[part, :share, :] = far_tile_ref[at, :]
        out_ref[part, share : 2 * share, :] = tile[at]
        out_ref[part, 2 * share :, :] = rows


def own_residual(own, covariates, total):
    samples, width = own[0].shape
    padded = total.shape[0]
    return pl.pallas_call(
        functools.partial(own_kernel, covariates[0].shape[0] + 1),
        out_shape=(
            jax.ShapeDtypeStruct((padded, padded), F32),
            jax.ShapeDtypeStruct((6 * padded, 2 * samples), BF16),
            jax.ShapeDtypeStruct((2 * samples, width), BF16),
            jax.ShapeDtypeStruct((2, width), BF16),
        ),
        scratch_shapes=[pltpu.VMEM((padded, 2 * samples), F32)],
        compiler_params=pltpu.CompilerParams(vmem_limit_bytes=12 << 20),
        cost_estimate=pl.CostEstimate(flops=4_000_000_000, bytes_accessed=15_000_000, transcendentals=0),
        name="own_residual",
    )(*own, *covariates, total)


def far_tile(far, cross_far, solved, white, left, own_rows):
    samples, width = far[0].shape
    return pl.pallas_call(
        far_kernel,
        out_shape=(
            jax.ShapeDtypeStruct((width, width), BF16),
            jax.ShapeDtypeStruct((4, width), BF16),
        ),
        scratch_shapes=[pltpu.VMEM((2 * samples, width), BF16)],
        compiler_params=pltpu.CompilerParams(vmem_limit_bytes=12 << 20),
        cost_estimate=pl.CostEstimate(flops=1_000_000_000, bytes_accessed=6_000_000, transcendentals=0),
        name="far_tile",
    )(*far, cross_far, solved, white, left, own_rows)


def messages(near, cross_near, solved, far, left, white, rows, parts):
    samples, width = near[0].shape
    return pl.pallas_call(
        near_kernel,
        out_shape=jax.ShapeDtypeStruct((parts, 2 * (width // parts) + 8, width), BF16),
        scratch_shapes=[pltpu.VMEM((2 * samples, width), BF16)],
        compiler_params=pltpu.CompilerParams(vmem_limit_bytes=16 << 20),
        name="messages",
    )(*near, cross_near, solved, far, left, white, rows)


def bands_kernel(samples, where_ref, reach_ref, arrived_ref, out_ref):
    parts = arrived_ref.shape[0]
    share, width = out_ref.shape[1:]
    place = where_ref[0]
    reached = reach_ref[where_ref[1]]
    far, near, weights = [], [], []
    for side in range(2):
        whole = sum(arrived_ref[part].astype(F32) for part in range(side, parts, 2))
        far.append(whole[:share])
        near.append(whole[share : 2 * share])
        spread = [whole[at : at + 1] + whole[at + 1 : at + 2] for at in range(2 * share, 2 * share + 6, 2)]
        weights.append([jnp.sqrt(samples / value) for value in spread])
    row = lax.broadcasted_iota(jnp.int32, (share, width), 0)
    lane = lax.broadcasted_iota(jnp.int32, (share, width), 1)
    mine = lane == row + place * share
    own = jnp.sum(jnp.where(mine, weights[0][0], 0.0), 1, keepdims=True) * (1.0 / math.sqrt(samples))
    slots = [
        (far[1], weights[1][1], 2),
        (near[1], weights[1][2], 1),
        (near[0], weights[0][2], 1),
        (far[0], weights[0][1], 2),
    ]
    for slot, (total, weight, offset) in enumerate(slots):
        live = jnp.full((share, width), reached, jnp.int32) >= offset
        out_ref[slot] = jnp.where(live, total * own * weight, 0.0).astype(BF16)


def bands(where, reach, arrived, samples):
    parts, _, width = arrived.shape
    share = width // parts
    smem = pl.BlockSpec(memory_space=pltpu.SMEM)
    vmem = pl.BlockSpec(memory_space=pltpu.VMEM)
    return pl.pallas_call(
        functools.partial(bands_kernel, samples),
        out_shape=jax.ShapeDtypeStruct((2 * MAXR, share, width), BF16),
        in_specs=[smem, smem, vmem],
        out_specs=vmem,
        compiler_params=pltpu.CompilerParams(vmem_limit_bytes=8 << 20),
        name="bands",
    )(where, reach, arrived)


def exchange(x):
    return lax.all_to_all(x, "sample", 0, 0, tiled=False)


def shards(dosage, covariates, reach):
    local_samples, width = dosage.shape
    parts = lax.axis_size("sample")
    blocks = lax.axis_size("variant")
    half = parts // 2
    samples = local_samples * parts
    place = lax.axis_index("sample")
    core = lax.axis_index("variant") % 2
    side = place % 2
    padded = -(-(covariates.shape[0] + 1) // parts) * parts
    both = ("sample", "variant")

    partner_route = [(i, i ^ 1) for i in range(parts)]
    core_route = [(i, i ^ 1) for i in range(blocks)]
    far_route = []
    for s in range(parts):
        step = MAXR if s % 2 == 0 else -MAXR
        for v in range(blocks):
            far_route.append((s * blocks + (v + step) % blocks, s * blocks + v))

    def from_partner(x):
        return lax.ppermute(x, "sample", partner_route)

    def from_far(x):
        return lax.ppermute(x, both, far_route)

    def for_mate(own, far):
        return jnp.where(core != side, own, far)

    def swap(x):
        return lax.ppermute(x, "variant", core_route)

    def after(x, *earlier):
        return lax.optimization_barrier((x,) + earlier)[0]

    own0 = dosage
    covariates1 = from_partner(covariates)
    message = local_sums(dosage, covariates, padded, parts)
    sent = own0
    own1 = from_partner(sent)
    far0 = from_far(sent)
    chunk = exchange(message).sum(0)
    message = jnp.broadcast_to(chunk[None], (parts,) + chunk.shape)
    message = after(message, own1, far0)
    give0 = for_mate(after(own0, message), far0)
    far1 = from_far(after(own1, give0))
    total = exchange(message).reshape(padded, -1)
    near0, near1 = swap(give0), swap(for_mate(own1, far1))
    cross = total[:, :width]
    cross_far = from_far(cross)
    solved, white, left, own_rows = own_residual((own0, own1), (covariates, covariates1), total)
    cross_near = swap(for_mate(after(cross, left), cross_far))
    tile, spreads = far_tile((far0, far1), cross_far, solved, white, left, own_rows)
    message = messages((near0, near1), cross_near, solved, tile, left, white, spreads, parts)
    where = jnp.stack([place, lax.axis_index("variant")])
    return bands(where, reach, exchange(message), samples)


def solution(mesh):
    placed = (P("sample", "variant"), P(None, "sample"), P())
    return jax.shard_map(
        shards,
        mesh=mesh,
        in_specs=placed,
        out_specs=P(None, ("variant", "sample"), None),
        check_vma=False,
    )
```

```python
import functools
import math

import jax
import jax.numpy as jnp
from jax import lax
from jax.experimental import pallas as pl
from jax.experimental.pallas import tpu as pltpu
from jax.sharding import PartitionSpec as P

MAXR = 2
HIGHEST = lax.Precision.HIGHEST
BF16 = jnp.bfloat16
F32 = jnp.float32
LANES = 128
STEP = 128
COLUMNS_TOGETHER = (((0,), (0,)), ((), ()))


def split(value):
    high = value.astype(BF16)
    rest = value - high.astype(F32)
    middle = rest.astype(BF16)
    low = (rest - middle.astype(F32)).astype(BF16)
    return high, middle, low


def fill_design(design_ref, covariates_ref):
    count = covariates_ref.shape[0]
    design_ref[...] = jnp.zeros_like(design_ref)
    design_ref[:count, :] = covariates_ref[...]
    design_ref[count : count + 1, :] = jnp.ones((1, design_ref.shape[1]), F32)


def sums_kernel(dosage_ref, covariates_ref, out_ref, design_ref):
    fill_design(design_ref, covariates_ref)
    width = dosage_ref.shape[1]
    padded = design_ref.shape[0]
    design = design_ref[...]
    stacked = jnp.concatenate(split(design), 0)
    parts = jnp.dot(stacked, dosage_ref[...], preferred_element_type=F32)
    cross = parts[:padded] + parts[padded : 2 * padded] + parts[2 * padded :]
    moment = lax.dot_general(
        design, design, (((1,), (1,)), ((), ())), precision=HIGHEST, preferred_element_type=F32
    )
    packed = jnp.concatenate([moment[at : at + 8] for at in range(0, padded, 8)], 1)
    each = out_ref.shape[1]
    for part in range(out_ref.shape[0]):
        out_ref[part, :, :width] = cross[part * each : (part + 1) * each]
        for at in range(0, 8, each):
            first = width + at // each * LANES
            out_ref[part, :, first : first + LANES] = packed[at : at + each]


def local_sums(dosage, covariates, padded, parts):
    samples, width = dosage.shape
    return pl.pallas_call(
        sums_kernel,
        out_shape=jax.ShapeDtypeStruct((parts, padded // parts, width + 8 * LANES // (padded // parts)), F32),
        scratch_shapes=[pltpu.VMEM((padded, samples), F32)],
        name="local_sums",
    )(dosage, covariates)


def factor_kernel(count, sums_ref, cov0, cov1, solved_ref, white_ref, design):
    samples = cov0.shape[1]
    padded = solved_ref.shape[0]
    parts, each, total_width = sums_ref.shape
    width = total_width - 8 * LANES // each
    whole = sums_ref[0, :, width:]
    for part in range(1, parts):
        whole = whole + sums_ref[part, :, width:]
    packed = jnp.concatenate([whole[:, at : at + LANES] for at in range(0, whole.shape[1], LANES)], 0)
    first = LANES // 2
    moment = jnp.concatenate(
        [pltpu.roll(packed, (first - group * padded) % LANES, 1) for group in range(padded // 8)], 0
    )
    row = lax.broadcasted_iota(jnp.int32, (padded, LANES), 0)
    lane = lax.broadcasted_iota(jnp.int32, (padded, LANES), 1)
    spare = (row >= count) & (lane == row + first)
    inside = (lane >= first) & (lane < first + padded)
    work = jnp.where(inside, moment, 0.0) + jnp.where((lane == row) | spare, 1.0, 0.0)
    for step in range(count - 1):
        pivot_row = work[step : step + 1, :]
        pivot_row = pivot_row / pivot_row[:, first + step : first + step + 1]
        column = jnp.broadcast_to(work[:, first + step : first + step + 1], work.shape)
        work = work - jnp.where(row > step, column, 0.0) * pivot_row
    diagonal = jnp.sum(jnp.where(lane == row + first, work, 0.0), 1, keepdims=True)
    unit = work[:, :padded]
    solved_ref[...] = unit / diagonal
    fill_design(design.at[:, :samples], cov0)
    fill_design(design.at[:, samples:], cov1)
    h, m, l = split(jnp.dot(unit, design[...], precision=HIGHEST, preferred_element_type=F32))
    white_ref[...] = jnp.concatenate([h, h, m, h, l, m], 0)


def residual(pieces, cross, solved, white, target):
    h, m, l = split(jnp.dot(solved, cross, precision=HIGHEST, preferred_element_type=F32))
    stacked = jnp.concatenate([h, m, h, l, h, m], 0)
    spread = jnp.zeros((1, stacked.shape[1]), F32)
    at = 0
    for piece in pieces:
        for start in range(0, piece.shape[0], STEP):
            fitted = lax.dot_general(
                white[:, at : at + STEP], stacked, COLUMNS_TOGETHER, preferred_element_type=F32
            )
            rest = piece[start : start + STEP, :].astype(F32) - fitted
            spread = spread + jnp.sum(rest * rest, 0, keepdims=True)
            target[at : at + STEP, :] = rest.astype(BF16)
            at += STEP
    return [spread.astype(BF16)]


def tile_of(left, right):
    tile = lax.dot_general(left[...], right[...], COLUMNS_TOGETHER, preferred_element_type=F32)
    return tile.astype(BF16)


def own_kernel(own0, own1, cross, solved, white, left, rows_ref):
    rows = residual((own0, own1), cross[...], solved[...], white[...], left)
    rows_ref[...] = rows[0]


def tiles_kernel(
    far0, far1, near, cross_far, cross_near, solved, white, left, own_rows,
    out_ref, right, far_part, near_part, sems,
):
    width = far0.shape[1]
    parts = out_ref.shape[0]
    share = width // parts
    groups = range(0, width, LANES)
    tall = share * len(groups)

    def sent(buffer, first, count, row, sem):
        return pltpu.make_async_copy(
            buffer.at[first : first + count],
            out_ref.at[first : first + count, row : row + buffer.shape[1], :],
            sems.at[sem],
        )

    def place(tile, index, buffer, part):
        for group, lane in enumerate(groups):
            buffer[part, group * share : (group + 1) * share, :] = tile[
                index * share : (index + 1) * share, lane : lane + LANES
            ]

    rows = [own_rows[...]] + residual((far0, far1), cross_far[...], solved[...], white[...], right)
    tile = tile_of(left, right)
    for part in range(parts):
        place(tile, part, far_part, part)
    copies = [sent(far_part, 0, parts, 0, 0)]
    copies[0].start()
    rows += residual((near.at[0], near.at[1]), cross_near[...], solved[...], white[...], right)
    rows = jnp.concatenate(rows + [jnp.zeros((1, width), BF16)], 0)
    rows = jnp.concatenate([rows[:, lane : lane + LANES] for lane in groups], 0)
    half = parts // 2
    for group in range(2):
        tile = tile_of(left.at[:, group * half * share : (group + 1) * half * share], right)
        for index in range(half):
            part = group * half + index
            place(tile, index, near_part, part)
            near_part[part, tall:, :] = rows
        copies.append(sent(near_part, group * half, half, tall, 1 + group))
        copies[-1].start()
    for copy in copies:
        copy.wait()


def factored(sums, covariates, padded):
    count, samples = covariates[0].shape
    return pl.pallas_call(
        functools.partial(factor_kernel, count + 1),
        out_shape=(
            jax.ShapeDtypeStruct((padded, padded), F32),
            jax.ShapeDtypeStruct((6 * padded, 2 * samples), BF16),
        ),
        scratch_shapes=[pltpu.VMEM((padded, 2 * samples), F32)],
        compiler_params=pltpu.CompilerParams(vmem_limit_bytes=4 << 20),
        cost_estimate=pl.CostEstimate(flops=3_000_000_000, bytes_accessed=10_000_000, transcendentals=0),
        name="factored",
    )(sums, *covariates)


def own_residual(own, cross, solved, white):
    samples, width = own[0].shape
    return pl.pallas_call(
        own_kernel,
        out_shape=(
            jax.ShapeDtypeStruct((2 * samples, width), BF16),
            jax.ShapeDtypeStruct((1, width), BF16),
        ),
        compiler_params=pltpu.CompilerParams(vmem_limit_bytes=8 << 20),
        cost_estimate=pl.CostEstimate(flops=800_000_000, bytes_accessed=4_000_000, transcendentals=0),
        name="own_residual",
    )(*own, cross, solved, white)


def tiles(far, near, cross_far, cross_near, solved, white, left, own_rows, parts):
    samples, width = far[0].shape
    share = width // parts
    tall = share * width // LANES
    extra = 4 * width // LANES
    return pl.pallas_call(
        tiles_kernel,
        out_shape=jax.ShapeDtypeStruct((parts, 2 * tall + extra, LANES), BF16),
        out_specs=pl.BlockSpec(memory_space=pl.ANY),
        scratch_shapes=[
            pltpu.VMEM((2 * samples, width), BF16),
            pltpu.VMEM((parts, tall, LANES), BF16),
            pltpu.VMEM((parts, tall + extra, LANES), BF16),
            pltpu.SemaphoreType.DMA((3,)),
        ],
        compiler_params=pltpu.CompilerParams(vmem_limit_bytes=16 << 20),
        cost_estimate=pl.CostEstimate(flops=2_000_000_000, bytes_accessed=6_000_000, transcendentals=0),
        name="tiles",
    )(*far, near, cross_far, cross_near, solved, white, left, own_rows)


def bands_kernel(samples, where_ref, reach_ref, arrived_ref, out_ref):
    parts = arrived_ref.shape[0]
    share, width = out_ref.shape[1:]
    place = where_ref[0]
    reached = reach_ref[where_ref[1]]
    groups = width // LANES
    tall = share * groups

    def wide(rows, height):
        return jnp.concatenate([rows[g * height : (g + 1) * height] for g in range(groups)], 1)

    far, near, weights = [], [], []
    for side in range(2):
        whole = sum(arrived_ref[part].astype(F32) for part in range(side, parts, 2))
        far.append(wide(whole[:tall], share))
        near.append(wide(whole[tall : 2 * tall], share))
        spread = wide(whole[2 * tall :], 4)
        weights.append([jnp.sqrt(samples / spread[at : at + 1]) for at in range(3)])
    row = lax.broadcasted_iota(jnp.int32, (share, width), 0)
    lane = lax.broadcasted_iota(jnp.int32, (share, width), 1)
    mine = lane == row + place * share
    own = jnp.sum(jnp.where(mine, weights[0][0], 0.0), 1, keepdims=True) * (1.0 / math.sqrt(samples))
    slots = [
        (far[1], weights[1][1], 2),
        (near[1], weights[1][2], 1),
        (near[0], weights[0][2], 1),
        (far[0], weights[0][1], 2),
    ]
    for slot, (total, weight, offset) in enumerate(slots):
        live = jnp.full((share, width), reached, jnp.int32) >= offset
        out_ref[slot] = jnp.where(live, total * own * weight, 0.0).astype(BF16)


def bands(where, reach, arrived, samples, width):
    share = width // arrived.shape[0]
    smem = pl.BlockSpec(memory_space=pltpu.SMEM)
    vmem = pl.BlockSpec(memory_space=pltpu.VMEM)
    return pl.pallas_call(
        functools.partial(bands_kernel, samples),
        out_shape=jax.ShapeDtypeStruct((2 * MAXR, share, width), BF16),
        in_specs=[smem, smem, vmem],
        out_specs=vmem,
        compiler_params=pltpu.CompilerParams(vmem_limit_bytes=8 << 20),
        name="bands",
    )(where, reach, arrived)


def exchange(x):
    return lax.all_to_all(x, "sample", 0, 0, tiled=False)


def shards(dosage, covariates, reach):
    local_samples, width = dosage.shape
    parts = lax.axis_size("sample")
    blocks = lax.axis_size("variant")
    half = parts // 2
    samples = local_samples * parts
    place = lax.axis_index("sample")
    core = lax.axis_index("variant") % 2
    side = place % 2
    padded = -(-(covariates.shape[0] + 1) // parts) * parts
    both = ("sample", "variant")

    partner_route = [(i, i ^ 1) for i in range(parts)]
    core_route = [(i, i ^ 1) for i in range(blocks)]
    far_route = []
    near_route = []
    for s in range(parts):
        step = MAXR if s % 2 == 0 else -MAXR
        for v in range(blocks):
            far_route.append((s * blocks + (v + step) % blocks, s * blocks + v))
            near_route.append((s * blocks + (v + step // MAXR) % blocks, s * blocks + v))

    def from_partner(x):
        return lax.ppermute(x, "sample", partner_route)

    def from_far(x):
        return lax.ppermute(x, both, far_route)

    def for_mate(own, far):
        return jnp.where(core != side, own, far)

    def swap(x):
        return lax.ppermute(x, "variant", core_route)

    def after(x, *earlier):
        return lax.optimization_barrier((x,) + earlier)[0]

    own0 = dosage
    covariates1 = from_partner(covariates)
    message = local_sums(dosage, covariates, padded, parts)
    sent = own0
    own1 = from_partner(sent)
    far0 = from_far(sent)
    sums = exchange(message)
    chunk = sums[:, :, :width].sum(0)
    message = jnp.broadcast_to(chunk[None], (parts,) + chunk.shape)
    message = after(message, own1, far0, covariates1)
    far1 = from_far(after(own1, message))
    cross = exchange(message).reshape(padded, width)
    solved, white = factored(after(sums, message), (covariates, covariates1), padded)
    cross_far = from_far(cross)
    left, own_rows = own_residual((own0, own1), cross, solved, white)
    cross_near = lax.ppermute(cross, both, near_route)
    near = swap(after(for_mate(jnp.stack([own0, own1]), jnp.stack([far0, far1])), left))
    message = tiles(
        (far0, far1), near, cross_far, cross_near, solved, white, left, own_rows, parts
    )
    where = jnp.stack([place, lax.axis_index("variant")])
    return bands(where, reach, exchange(message), samples, width)


def solution(mesh):
    placed = (P("sample", "variant"), P(None, "sample"), P())
    return jax.shard_map(
        shards,
        mesh=mesh,
        in_specs=placed,
        out_specs=P(None, ("variant", "sample"), None),
        check_vma=False,
    )
```

```python
import functools
import math

import jax
import jax.numpy as jnp
from jax import lax
from jax.experimental import pallas as pl
from jax.experimental.pallas import tpu as pltpu
from jax.sharding import PartitionSpec as P

MAXR = 2
HIGHEST = lax.Precision.HIGHEST
BF16 = jnp.bfloat16
F32 = jnp.float32
LANES = 128
STEP = 256
COLUMNS_TOGETHER = (((0,), (0,)), ((), ()))


def split(value):
    high = value.astype(BF16)
    rest = value - high.astype(F32)
    middle = rest.astype(BF16)
    low = (rest - middle.astype(F32)).astype(BF16)
    return high, middle, low


def fill_design(design_ref, covariates_ref):
    count = covariates_ref.shape[0]
    design_ref[...] = jnp.zeros_like(design_ref)
    design_ref[:count, :] = covariates_ref[...]
    design_ref[count : count + 1, :] = jnp.ones((1, design_ref.shape[1]), F32)


def sums_kernel(dosage_ref, covariates_ref, out_ref, design_ref):
    fill_design(design_ref, covariates_ref)
    width = dosage_ref.shape[1]
    padded = design_ref.shape[0]
    design = design_ref[...]
    stacked = jnp.concatenate(split(design), 0)
    parts = jnp.dot(stacked, dosage_ref[...], preferred_element_type=F32)
    cross = parts[:padded] + parts[padded : 2 * padded] + parts[2 * padded :]
    moment = lax.dot_general(
        design, design, (((1,), (1,)), ((), ())), precision=HIGHEST, preferred_element_type=F32
    )
    packed = jnp.concatenate([moment[at : at + 8] for at in range(0, padded, 8)], 1)
    each = out_ref.shape[1]
    for part in range(out_ref.shape[0]):
        out_ref[part, :, :width] = cross[part * each : (part + 1) * each]
        for at in range(0, 8, each):
            first = width + at // each * LANES
            out_ref[part, :, first : first + LANES] = packed[at : at + each]


def local_sums(dosage, covariates, padded, parts):
    samples, width = dosage.shape
    return pl.pallas_call(
        sums_kernel,
        out_shape=jax.ShapeDtypeStruct((parts, padded // parts, width + 8 * LANES // (padded // parts)), F32),
        scratch_shapes=[pltpu.VMEM((padded, samples), F32)],
        name="local_sums",
    )(dosage, covariates)


def factor_kernel(count, sums_ref, cov0, cov1, solved_ref, white_ref, design):
    samples = cov0.shape[1]
    padded = solved_ref.shape[0]
    parts, each, total_width = sums_ref.shape
    width = total_width - 8 * LANES // each
    whole = sums_ref[0, :, width:]
    for part in range(1, parts):
        whole = whole + sums_ref[part, :, width:]
    packed = jnp.concatenate([whole[:, at : at + LANES] for at in range(0, whole.shape[1], LANES)], 0)
    first = LANES // 2
    moment = jnp.concatenate(
        [pltpu.roll(packed, (first - group * padded) % LANES, 1) for group in range(padded // 8)], 0
    )
    row = lax.broadcasted_iota(jnp.int32, (padded, LANES), 0)
    lane = lax.broadcasted_iota(jnp.int32, (padded, LANES), 1)
    spare = (row >= count) & (lane == row + first)
    inside = (lane >= first) & (lane < first + padded)
    work = jnp.where(inside, moment, 0.0) + jnp.where((lane == row) | spare, 1.0, 0.0)
    for step in range(count - 1):
        pivot_row = work[step : step + 1, :]
        pivot_row = pivot_row / pivot_row[:, first + step : first + step + 1]
        column = jnp.broadcast_to(work[:, first + step : first + step + 1], work.shape)
        work = work - jnp.where(row > step, column, 0.0) * pivot_row
    diagonal = jnp.sum(jnp.where(lane == row + first, work, 0.0), 1, keepdims=True)
    unit = work[:, :padded]
    solved_ref[...] = unit / diagonal
    fill_design(design.at[:, :samples], cov0)
    fill_design(design.at[:, samples:], cov1)
    h, m, l = split(jnp.dot(unit, design[...], precision=HIGHEST, preferred_element_type=F32))
    white_ref[...] = jnp.concatenate([h, h, m, h, l, m], 0)


def residual(pieces, cross, solved, white, target):
    h, m, l = split(jnp.dot(solved, cross, precision=HIGHEST, preferred_element_type=F32))
    stacked = jnp.concatenate([h, m, h, l, h, m], 0)
    spread = jnp.zeros((1, stacked.shape[1]), F32)
    at = 0
    for piece in pieces:
        for start in range(0, piece.shape[0], STEP):
            fitted = lax.dot_general(
                white[:, at : at + STEP], stacked, COLUMNS_TOGETHER, preferred_element_type=F32
            )
            rest = piece[start : start + STEP, :].astype(F32) - fitted
            spread = spread + jnp.sum(rest * rest, 0, keepdims=True)
            target[at : at + STEP, :] = rest.astype(BF16)
            at += STEP
    return [spread.astype(BF16)]


def tile_of(left, right):
    tile = lax.dot_general(left[...], right[...], COLUMNS_TOGETHER, preferred_element_type=F32)
    return tile.astype(BF16)


def own_kernel(own0, own1, cross, solved, white, left, rows_ref):
    rows = residual((own0, own1), cross[...], solved[...], white[...], left)
    rows_ref[...] = rows[0]


def tiles_kernel(
    far0, far1, near, cross_far, cross_near, solved, white, left, own_rows,
    out_ref, right, far_part, near_part, sems,
):
    width = far0.shape[1]
    parts = out_ref.shape[0]
    share = width // parts
    groups = range(0, width, LANES)
    tall = share * len(groups)

    def sent(buffer, first, count, row, sem):
        return pltpu.make_async_copy(
            buffer.at[first : first + count],
            out_ref.at[first : first + count, row : row + buffer.shape[1], :],
            sems.at[sem],
        )

    def place(tile, index, buffer, part):
        for group, lane in enumerate(groups):
            buffer[part, group * share : (group + 1) * share, :] = tile[
                index * share : (index + 1) * share, lane : lane + LANES
            ]

    rows = [own_rows[...]] + residual((far0, far1), cross_far[...], solved[...], white[...], right)
    tile = tile_of(left, right)
    for part in range(parts):
        place(tile, part, far_part, part)
    copies = [sent(far_part, 0, parts, 0, 0)]
    copies[0].start()
    rows += residual((near.at[0], near.at[1]), cross_near[...], solved[...], white[...], right)
    rows = jnp.concatenate(rows + [jnp.zeros((1, width), BF16)], 0)
    rows = jnp.concatenate([rows[:, lane : lane + LANES] for lane in groups], 0)
    half = parts // 2
    for group in range(2):
        tile = tile_of(left.at[:, group * half * share : (group + 1) * half * share], right)
        for index in range(half):
            part = group * half + index
            place(tile, index, near_part, part)
            near_part[part, tall:, :] = rows
        copies.append(sent(near_part, group * half, half, tall, 1 + group))
        copies[-1].start()
    for copy in copies:
        copy.wait()


def factored(sums, covariates, padded):
    count, samples = covariates[0].shape
    return pl.pallas_call(
        functools.partial(factor_kernel, count + 1),
        out_shape=(
            jax.ShapeDtypeStruct((padded, padded), F32),
            jax.ShapeDtypeStruct((6 * padded, 2 * samples), BF16),
        ),
        scratch_shapes=[pltpu.VMEM((padded, 2 * samples), F32)],
        compiler_params=pltpu.CompilerParams(vmem_limit_bytes=4 << 20),
        cost_estimate=pl.CostEstimate(flops=3_000_000_000, bytes_accessed=10_000_000, transcendentals=0),
        name="factored",
    )(sums, *covariates)


def own_residual(own, cross, solved, white):
    samples, width = own[0].shape
    return pl.pallas_call(
        own_kernel,
        out_shape=(
            jax.ShapeDtypeStruct((2 * samples, width), BF16),
            jax.ShapeDtypeStruct((1, width), BF16),
        ),
        compiler_params=pltpu.CompilerParams(vmem_limit_bytes=8 << 20),
        cost_estimate=pl.CostEstimate(flops=800_000_000, bytes_accessed=4_000_000, transcendentals=0),
        name="own_residual",
    )(*own, cross, solved, white)


def tiles(far, near, cross_far, cross_near, solved, white, left, own_rows, parts):
    samples, width = far[0].shape
    share = width // parts
    tall = share * width // LANES
    extra = 4 * width // LANES
    return pl.pallas_call(
        tiles_kernel,
        out_shape=jax.ShapeDtypeStruct((parts, 2 * tall + extra, LANES), BF16),
        out_specs=pl.BlockSpec(memory_space=pl.ANY),
        scratch_shapes=[
            pltpu.VMEM((2 * samples, width), BF16),
            pltpu.VMEM((parts, tall, LANES), BF16),
            pltpu.VMEM((parts, tall + extra, LANES), BF16),
            pltpu.SemaphoreType.DMA((3,)),
        ],
        compiler_params=pltpu.CompilerParams(vmem_limit_bytes=16 << 20),
        cost_estimate=pl.CostEstimate(flops=2_000_000_000, bytes_accessed=6_000_000, transcendentals=0),
        name="tiles",
    )(*far, near, cross_far, cross_near, solved, white, left, own_rows)


def bands_kernel(samples, marks_ref, arrived_ref, out_ref):
    parts = arrived_ref.shape[0]
    share, width = out_ref.shape[1:]
    groups = width // LANES
    tall = share * groups

    def wide(rows, height):
        return jnp.concatenate([rows[g * height : (g + 1) * height] for g in range(groups)], 1)

    far, near, weights = [], [], []
    for side in range(2):
        whole = sum(arrived_ref[part].astype(F32) for part in range(side, parts, 2))
        far.append(wide(whole[:tall], share))
        near.append(wide(whole[tall : 2 * tall], share))
        spread = wide(whole[2 * tall :], 4)
        weights.append([jnp.sqrt(samples / spread[at : at + 1]) for at in range(3)])
    row = lax.broadcasted_iota(jnp.int32, (share, width), 0)
    mine = row == marks_ref[0:1, :]
    reached = marks_ref[1:2, :]
    own = jnp.sum(jnp.where(mine, weights[0][0], 0.0), 1, keepdims=True) * (1.0 / math.sqrt(samples))
    slots = [
        (far[1], weights[1][1], 2),
        (near[1], weights[1][2], 1),
        (near[0], weights[0][2], 1),
        (far[0], weights[0][1], 2),
    ]
    for slot, (total, weight, offset) in enumerate(slots):
        live = reached >= offset
        out_ref[slot] = jnp.where(live, total * own * weight, 0.0).astype(BF16)


def bands(marks, arrived, samples, width):
    share = width // arrived.shape[0]
    vmem = pl.BlockSpec(memory_space=pltpu.VMEM)
    return pl.pallas_call(
        functools.partial(bands_kernel, samples),
        out_shape=jax.ShapeDtypeStruct((2 * MAXR, share, width), BF16),
        in_specs=[vmem, vmem],
        out_specs=vmem,
        compiler_params=pltpu.CompilerParams(vmem_limit_bytes=8 << 20),
        name="bands",
    )(marks, arrived)


def exchange(x):
    return lax.all_to_all(x, "sample", 0, 0, tiled=False)


def shards(dosage, covariates, reach):
    local_samples, width = dosage.shape
    parts = lax.axis_size("sample")
    blocks = lax.axis_size("variant")
    half = parts // 2
    samples = local_samples * parts
    place = lax.axis_index("sample")
    core = lax.axis_index("variant") % 2
    side = place % 2
    padded = -(-(covariates.shape[0] + 1) // parts) * parts
    both = ("sample", "variant")

    partner_route = [(i, i ^ 1) for i in range(parts)]
    core_route = [(i, i ^ 1) for i in range(blocks)]
    far_route = []
    near_route = []
    for s in range(parts):
        step = MAXR if s % 2 == 0 else -MAXR
        for v in range(blocks):
            far_route.append((s * blocks + (v + step) % blocks, s * blocks + v))
            near_route.append((s * blocks + (v + step // MAXR) % blocks, s * blocks + v))

    def from_partner(x):
        return lax.ppermute(x, "sample", partner_route)

    def from_far(x):
        return lax.ppermute(x, both, far_route)

    def for_mate(own, far):
        return jnp.where(core != side, own, far)

    def swap(x):
        return lax.ppermute(x, "variant", core_route)

    def after(x, *earlier):
        return lax.optimization_barrier((x,) + earlier)[0]

    own0 = dosage
    covariates1 = from_partner(covariates)
    reached = reach[lax.axis_index("variant")]
    lanes = jnp.arange(width, dtype=jnp.int32) - place * (width // parts)
    marks = jnp.stack([lanes, jnp.full((width,), reached, jnp.int32)])
    message = local_sums(dosage, covariates, padded, parts)
    sent = own0
    own1 = from_partner(sent)
    far0 = from_far(sent)
    sums = exchange(message)
    chunk = sums[:, :, :width].sum(0)
    message = jnp.broadcast_to(chunk[None], (parts,) + chunk.shape)
    message = after(message, own1, far0, covariates1, marks)
    far1 = from_far(after(own1, message))
    cross = exchange(message).reshape(padded, width)
    solved, white = factored(after(sums, message), (covariates, covariates1), padded)
    cross_far = from_far(cross)
    left, own_rows = own_residual((own0, after(own1, far1)), cross, solved, white)
    cross_near = lax.ppermute(cross, both, near_route)
    near = swap(after(for_mate(jnp.stack([own0, own1]), jnp.stack([far0, far1])), left))
    message = tiles(
        (far0, far1), near, cross_far, cross_near, solved, white, left, own_rows, parts
    )
    return bands(marks, exchange(message), samples, width)


def solution(mesh):
    placed = (P("sample", "variant"), P(None, "sample"), P())
    return jax.shard_map(
        shards,
        mesh=mesh,
        in_specs=placed,
        out_specs=P(None, ("variant", "sample"), None),
        check_vma=False,
    )
```

```python
import functools
import math

import jax
import jax.numpy as jnp
from jax import lax
from jax.experimental import pallas as pl
from jax.experimental.pallas import tpu as pltpu
from jax.sharding import PartitionSpec as P

MAXR = 2
HIGHEST = lax.Precision.HIGHEST
BF16 = jnp.bfloat16
F32 = jnp.float32
LANES = 128
STEP = 128
COLUMNS_TOGETHER = (((0,), (0,)), ((), ()))


def split(value):
    high = value.astype(BF16)
    rest = value - high.astype(F32)
    middle = rest.astype(BF16)
    low = (rest - middle.astype(F32)).astype(BF16)
    return high, middle, low


def fill_design(design_ref, covariates_ref):
    count = covariates_ref.shape[0]
    design_ref[...] = jnp.zeros_like(design_ref)
    design_ref[:count, :] = covariates_ref[...]
    design_ref[count : count + 1, :] = jnp.ones((1, design_ref.shape[1]), F32)


def sums_kernel(dosage_hbm, covariates_hbm, out_ref, design_ref, dosage_ref, covariates_ref, sems):
    dosage_copy = pltpu.make_async_copy(dosage_hbm, dosage_ref, sems.at[0])
    covariates_copy = pltpu.make_async_copy(covariates_hbm, covariates_ref, sems.at[1])
    dosage_copy.start()
    covariates_copy.start()
    covariates_copy.wait()
    fill_design(design_ref, covariates_ref)
    width = dosage_ref.shape[1]
    padded = design_ref.shape[0]
    design = design_ref[...]
    stacked = jnp.concatenate(split(design), 0)
    moment = lax.dot_general(
        design, design, (((1,), (1,)), ((), ())), precision=HIGHEST, preferred_element_type=F32
    )
    dosage_copy.wait()
    parts = jnp.dot(stacked, dosage_ref[...], preferred_element_type=F32)
    cross = parts[:padded] + parts[padded : 2 * padded] + parts[2 * padded :]
    packed = jnp.concatenate([moment[at : at + 8] for at in range(0, padded, 8)], 1)
    each = out_ref.shape[1]
    for part in range(out_ref.shape[0]):
        out_ref[part, :, :width] = cross[part * each : (part + 1) * each]
        for at in range(0, 8, each):
            first = width + at // each * LANES
            out_ref[part, :, first : first + LANES] = packed[at : at + each]


def local_sums(dosage, covariates, padded, parts):
    samples, width = dosage.shape
    return pl.pallas_call(
        sums_kernel,
        out_shape=jax.ShapeDtypeStruct((parts, padded // parts, width + 8 * LANES // (padded // parts)), F32),
        in_specs=[pl.BlockSpec(memory_space=pl.ANY)] * 2,
        scratch_shapes=[
            pltpu.VMEM((padded, samples), F32),
            pltpu.VMEM(dosage.shape, BF16),
            pltpu.VMEM(covariates.shape, F32),
            pltpu.SemaphoreType.DMA((2,)),
        ],
        name="local_sums",
    )(dosage, covariates)


def factor_kernel(count, sums_ref, cov0, cov1, solved_ref, white_ref, design):
    samples = cov0.shape[1]
    padded = solved_ref.shape[0]
    parts, each, total_width = sums_ref.shape
    width = total_width - 8 * LANES // each
    whole = sums_ref[0, :, width:]
    for part in range(1, parts):
        whole = whole + sums_ref[part, :, width:]
    packed = jnp.concatenate([whole[:, at : at + LANES] for at in range(0, whole.shape[1], LANES)], 0)
    first = LANES // 2
    moment = jnp.concatenate(
        [pltpu.roll(packed, (first - group * padded) % LANES, 1) for group in range(padded // 8)], 0
    )
    row = lax.broadcasted_iota(jnp.int32, (padded, LANES), 0)
    lane = lax.broadcasted_iota(jnp.int32, (padded, LANES), 1)
    spare = (row >= count) & (lane == row + first)
    inside = (lane >= first) & (lane < first + padded)
    work = jnp.where(inside, moment, 0.0) + jnp.where((lane == row) | spare, 1.0, 0.0)
    for step in range(count - 1):
        pivot_row = work[step : step + 1, :]
        pivot_row = pivot_row / pivot_row[:, first + step : first + step + 1]
        column = jnp.broadcast_to(work[:, first + step : first + step + 1], work.shape)
        work = work - jnp.where(row > step, column, 0.0) * pivot_row
    diagonal = jnp.sum(jnp.where(lane == row + first, work, 0.0), 1, keepdims=True)
    unit = work[:, :padded]
    solved_ref[...] = unit / diagonal
    fill_design(design.at[:, :samples], cov0)
    fill_design(design.at[:, samples:], cov1)
    h, m, l = split(jnp.dot(unit, design[...], precision=HIGHEST, preferred_element_type=F32))
    white_ref[...] = jnp.concatenate([h, h, m, h, l, m], 0)


def residual(pieces, cross, solved, white, target):
    h, m, l = split(jnp.dot(solved, cross, precision=HIGHEST, preferred_element_type=F32))
    stacked = jnp.concatenate([h, m, h, l, h, m], 0)
    spread = jnp.zeros((1, stacked.shape[1]), F32)
    at = 0
    for piece in pieces:
        for start in range(0, piece.shape[0], STEP):
            fitted = lax.dot_general(
                white[:, at : at + STEP], stacked, COLUMNS_TOGETHER, preferred_element_type=F32
            )
            rest = piece[start : start + STEP, :].astype(F32) - fitted
            spread = spread + jnp.sum(rest * rest, 0, keepdims=True)
            target[at : at + STEP, :] = rest.astype(BF16)
            at += STEP
    return [spread.astype(BF16)]


def tile_of(left, right):
    tile = lax.dot_general(left[...], right[...], COLUMNS_TOGETHER, preferred_element_type=F32)
    return tile.astype(BF16)


def own_kernel(own0, own1, cross, solved, white, left, rows_ref):
    rows = residual((own0, own1), cross[...], solved[...], white[...], left)
    rows_ref[...] = rows[0]


def tiles_kernel(
    far0, far1, near, cross_far, cross_near, solved, white, left, own_rows,
    out_ref, right, far_part, near_part, sems,
):
    width = far0.shape[1]
    parts = out_ref.shape[0]
    share = width // parts
    groups = range(0, width, LANES)
    tall = share * len(groups)

    def sent(buffer, first, count, row, sem):
        return pltpu.make_async_copy(
            buffer.at[first : first + count],
            out_ref.at[first : first + count, row : row + buffer.shape[1], :],
            sems.at[sem],
        )

    def place(tile, index, buffer, part):
        for group, lane in enumerate(groups):
            buffer[part, group * share : (group + 1) * share, :] = tile[
                index * share : (index + 1) * share, lane : lane + LANES
            ]

    rows = [own_rows[...]] + residual((far0, far1), cross_far[...], solved[...], white[...], right)
    tile = tile_of(left, right)
    for part in range(parts):
        place(tile, part, far_part, part)
    copies = [sent(far_part, 0, parts, 0, 0)]
    copies[0].start()
    rows += residual((near.at[0], near.at[1]), cross_near[...], solved[...], white[...], right)
    rows = jnp.concatenate(rows + [jnp.zeros((1, width), BF16)], 0)
    rows = jnp.concatenate([rows[:, lane : lane + LANES] for lane in groups], 0)
    half = parts // 2
    for group in range(2):
        tile = tile_of(left.at[:, group * half * share : (group + 1) * half * share], right)
        for index in range(half):
            part = group * half + index
            place(tile, index, near_part, part)
            near_part[part, tall:, :] = rows
        copies.append(sent(near_part, group * half, half, tall, 1 + group))
        copies[-1].start()
    for copy in copies:
        copy.wait()


def factored(sums, covariates, padded):
    count, samples = covariates[0].shape
    return pl.pallas_call(
        functools.partial(factor_kernel, count + 1),
        out_shape=(
            jax.ShapeDtypeStruct((padded, padded), F32),
            jax.ShapeDtypeStruct((6 * padded, 2 * samples), BF16),
        ),
        scratch_shapes=[pltpu.VMEM((padded, 2 * samples), F32)],
        compiler_params=pltpu.CompilerParams(vmem_limit_bytes=4 << 20),
        cost_estimate=pl.CostEstimate(flops=3_000_000_000, bytes_accessed=10_000_000, transcendentals=0),
        name="factored",
    )(sums, *covariates)


def own_residual(own, cross, solved, white):
    samples, width = own[0].shape
    return pl.pallas_call(
        own_kernel,
        out_shape=(
            jax.ShapeDtypeStruct((2 * samples, width), BF16),
            jax.ShapeDtypeStruct((1, width), BF16),
        ),
        compiler_params=pltpu.CompilerParams(vmem_limit_bytes=8 << 20),
        cost_estimate=pl.CostEstimate(flops=800_000_000, bytes_accessed=4_000_000, transcendentals=0),
        name="own_residual",
    )(*own, cross, solved, white)


def tiles(far, near, cross_far, cross_near, solved, white, left, own_rows, parts):
    samples, width = far[0].shape
    share = width // parts
    tall = share * width // LANES
    extra = 4 * width // LANES
    return pl.pallas_call(
        tiles_kernel,
        out_shape=jax.ShapeDtypeStruct((parts, 2 * tall + extra, LANES), BF16),
        out_specs=pl.BlockSpec(memory_space=pl.ANY),
        scratch_shapes=[
            pltpu.VMEM((2 * samples, width), BF16),
            pltpu.VMEM((parts, tall, LANES), BF16),
            pltpu.VMEM((parts, tall + extra, LANES), BF16),
            pltpu.SemaphoreType.DMA((3,)),
        ],
        compiler_params=pltpu.CompilerParams(vmem_limit_bytes=16 << 20),
        cost_estimate=pl.CostEstimate(flops=2_000_000_000, bytes_accessed=6_000_000, transcendentals=0),
        name="tiles",
    )(*far, near, cross_far, cross_near, solved, white, left, own_rows)


def bands_kernel(samples, where_ref, reach_ref, arrived_ref, out_ref):
    parts = arrived_ref.shape[0]
    share, width = out_ref.shape[1:]
    place = where_ref[0]
    reached = reach_ref[where_ref[1]]
    groups = width // LANES
    tall = share * groups

    def wide(rows, height):
        return jnp.concatenate([rows[g * height : (g + 1) * height] for g in range(groups)], 1)

    far, near, weights = [], [], []
    for side in range(2):
        whole = sum(arrived_ref[part].astype(F32) for part in range(side, parts, 2))
        far.append(wide(whole[:tall], share))
        near.append(wide(whole[tall : 2 * tall], share))
        spread = wide(whole[2 * tall :], 4)
        weights.append([jnp.sqrt(samples / spread[at : at + 1]) for at in range(3)])
    row = lax.broadcasted_iota(jnp.int32, (share, width), 0)
    lane = lax.broadcasted_iota(jnp.int32, (share, width), 1)
    mine = lane == row + place * share
    own = jnp.sum(jnp.where(mine, weights[0][0], 0.0), 1, keepdims=True) * (1.0 / math.sqrt(samples))
    slots = [
        (far[1], weights[1][1], 2),
        (near[1], weights[1][2], 1),
        (near[0], weights[0][2], 1),
        (far[0], weights[0][1], 2),
    ]
    for slot, (total, weight, offset) in enumerate(slots):
        live = jnp.full((share, width), reached, jnp.int32) >= offset
        out_ref[slot] = jnp.where(live, total * own * weight, 0.0).astype(BF16)


def bands(where, reach, arrived, samples, width):
    share = width // arrived.shape[0]
    smem = pl.BlockSpec(memory_space=pltpu.SMEM)
    vmem = pl.BlockSpec(memory_space=pltpu.VMEM)
    return pl.pallas_call(
        functools.partial(bands_kernel, samples),
        out_shape=jax.ShapeDtypeStruct((2 * MAXR, share, width), BF16),
        in_specs=[smem, smem, vmem],
        out_specs=vmem,
        compiler_params=pltpu.CompilerParams(vmem_limit_bytes=8 << 20),
        name="bands",
    )(where, reach, arrived)


def exchange(x):
    return lax.all_to_all(x, "sample", 0, 0, tiled=False)


def shards(dosage, covariates, reach):
    local_samples, width = dosage.shape
    parts = lax.axis_size("sample")
    blocks = lax.axis_size("variant")
    half = parts // 2
    samples = local_samples * parts
    place = lax.axis_index("sample")
    core = lax.axis_index("variant") % 2
    side = place % 2
    padded = -(-(covariates.shape[0] + 1) // parts) * parts
    both = ("sample", "variant")

    partner_route = [(i, i ^ 1) for i in range(parts)]
    core_route = [(i, i ^ 1) for i in range(blocks)]
    far_route = []
    near_route = []
    for s in range(parts):
        step = MAXR if s % 2 == 0 else -MAXR
        for v in range(blocks):
            far_route.append((s * blocks + (v + step) % blocks, s * blocks + v))
            near_route.append((s * blocks + (v + step // MAXR) % blocks, s * blocks + v))

    def from_partner(x):
        return lax.ppermute(x, "sample", partner_route)

    def from_far(x):
        return lax.ppermute(x, both, far_route)

    def for_mate(own, far):
        return jnp.where(core != side, own, far)

    def swap(x):
        return lax.ppermute(x, "variant", core_route)

    def after(x, *earlier):
        return lax.optimization_barrier((x,) + earlier)[0]

    own0 = dosage
    covariates1 = from_partner(covariates)
    message = local_sums(dosage, covariates, padded, parts)
    sent = own0
    own1 = from_partner(sent)
    far0 = from_far(sent)
    sums = exchange(message)
    chunk = sums[:, :, :width].sum(0)
    message = jnp.broadcast_to(chunk[None], (parts,) + chunk.shape)
    message = after(message, own1, far0, covariates1)
    far1 = from_far(after(own1, message))
    cross = exchange(message).reshape(padded, width)
    solved, white = factored(after(sums, message), (covariates, covariates1), padded)
    cross_far = from_far(cross)
    left, own_rows = own_residual((own0, own1), cross, solved, white)
    cross_near = lax.ppermute(cross, both, near_route)
    near = swap(after(for_mate(jnp.stack([own0, own1]), jnp.stack([far0, far1])), left))
    message = tiles(
        (far0, far1), near, cross_far, cross_near, solved, white, left, own_rows, parts
    )
    where = jnp.stack([place, lax.axis_index("variant")])
    return bands(where, reach, exchange(message), samples, width)


def solution(mesh):
    placed = (P("sample", "variant"), P(None, "sample"), P())
    return jax.shard_map(
        shards,
        mesh=mesh,
        in_specs=placed,
        out_specs=P(None, ("variant", "sample"), None),
        check_vma=False,
    )
```

```python
import functools
import math

import jax
import jax.numpy as jnp
from jax import lax
from jax.experimental import pallas as pl
from jax.experimental.pallas import tpu as pltpu
from jax.sharding import PartitionSpec as P

MAXR = 2
HIGHEST = lax.Precision.HIGHEST
BF16 = jnp.bfloat16
F32 = jnp.float32
LANES = 128
STEP = 128
COLUMNS_TOGETHER = (((0,), (0,)), ((), ()))


def split(value):
    high = value.astype(BF16)
    rest = value - high.astype(F32)
    middle = rest.astype(BF16)
    low = (rest - middle.astype(F32)).astype(BF16)
    return high, middle, low


def fill_design(design_ref, covariates_ref):
    count = covariates_ref.shape[0]
    design_ref[...] = jnp.zeros_like(design_ref)
    design_ref[:count, :] = covariates_ref[...]
    design_ref[count : count + 1, :] = jnp.ones((1, design_ref.shape[1]), F32)


def sums_kernel(dosage_ref, covariates_ref, out_ref, design_ref):
    fill_design(design_ref, covariates_ref)
    width = dosage_ref.shape[1]
    padded = design_ref.shape[0]
    design = design_ref[...]
    stacked = jnp.concatenate(split(design), 0)
    parts = jnp.dot(stacked, dosage_ref[...], preferred_element_type=F32)
    cross = parts[:padded] + parts[padded : 2 * padded] + parts[2 * padded :]
    moment = lax.dot_general(
        design, design, (((1,), (1,)), ((), ())), precision=HIGHEST, preferred_element_type=F32
    )
    packed = jnp.concatenate([moment[at : at + 8] for at in range(0, padded, 8)], 1)
    each = out_ref.shape[1]
    for part in range(out_ref.shape[0]):
        out_ref[part, :, :width] = cross[part * each : (part + 1) * each]
        for at in range(0, 8, each):
            first = width + at // each * LANES
            out_ref[part, :, first : first + LANES] = packed[at : at + each]


def local_sums(dosage, covariates, padded, parts):
    samples, width = dosage.shape
    return pl.pallas_call(
        sums_kernel,
        out_shape=jax.ShapeDtypeStruct((parts, padded // parts, width + 8 * LANES // (padded // parts)), F32),
        scratch_shapes=[pltpu.VMEM((padded, samples), F32)],
        name="local_sums",
    )(dosage, covariates)


def factor_kernel(count, sums_ref, cov0, cov1, solved_ref, white_ref, design):
    samples = cov0.shape[1]
    padded = solved_ref.shape[0]
    parts, each, total_width = sums_ref.shape
    width = total_width - 8 * LANES // each
    whole = sums_ref[0, :, width:]
    for part in range(1, parts):
        whole = whole + sums_ref[part, :, width:]
    packed = jnp.concatenate([whole[:, at : at + LANES] for at in range(0, whole.shape[1], LANES)], 0)
    first = LANES // 2
    moment = jnp.concatenate(
        [pltpu.roll(packed, (first - group * padded) % LANES, 1) for group in range(padded // 8)], 0
    )
    row = lax.broadcasted_iota(jnp.int32, (padded, LANES), 0)
    lane = lax.broadcasted_iota(jnp.int32, (padded, LANES), 1)
    spare = (row >= count) & (lane == row + first)
    inside = (lane >= first) & (lane < first + padded)
    work = jnp.where(inside, moment, 0.0) + jnp.where((lane == row) | spare, 1.0, 0.0)
    for step in range(count - 1):
        pivot_row = work[step : step + 1, :]
        pivot_row = pivot_row / pivot_row[:, first + step : first + step + 1]
        column = jnp.broadcast_to(work[:, first + step : first + step + 1], work.shape)
        work = work - jnp.where(row > step, column, 0.0) * pivot_row
    diagonal = jnp.sum(jnp.where(lane == row + first, work, 0.0), 1, keepdims=True)
    unit = work[:, :padded]
    solved_ref[...] = unit / diagonal
    fill_design(design.at[:, :samples], cov0)
    fill_design(design.at[:, samples:], cov1)
    h, m, l = split(jnp.dot(unit, design[...], precision=HIGHEST, preferred_element_type=F32))
    white_ref[...] = jnp.concatenate([h, h, m, h, l, m], 0)


def residual(pieces, cross, solved, white, target):
    h, m, l = split(jnp.dot(solved, cross, precision=HIGHEST, preferred_element_type=F32))
    stacked = jnp.concatenate([h, m, h, l, h, m], 0)
    spread = jnp.zeros((1, stacked.shape[1]), F32)
    at = 0
    for piece in pieces:
        for start in range(0, piece.shape[0], STEP):
            fitted = lax.dot_general(
                white[:, at : at + STEP], stacked, COLUMNS_TOGETHER, preferred_element_type=F32
            )
            rest = piece[start : start + STEP, :].astype(F32) - fitted
            spread = spread + jnp.sum(rest * rest, 0, keepdims=True)
            target[at : at + STEP, :] = rest.astype(BF16)
            at += STEP
    return [spread.astype(BF16)]


def tile_of(left, right):
    tile = lax.dot_general(left[...], right[...], COLUMNS_TOGETHER, preferred_element_type=F32)
    return tile.astype(BF16)


def own_kernel(own0, own1, cross, solved, white, left, rows_ref):
    rows = residual((own0, own1), cross[...], solved[...], white[...], left)
    rows_ref[...] = rows[0]


def tiles_kernel(
    far0, far1, near, cross_far, cross_near, solved, white, left, own_rows,
    out_ref, right, far_part, near_part, sems,
):
    width = far0.shape[1]
    parts = out_ref.shape[0]
    share = width // parts
    groups = range(0, width, LANES)
    tall = share * len(groups)

    def sent(buffer, first, count, row, sem):
        return pltpu.make_async_copy(
            buffer.at[first : first + count],
            out_ref.at[first : first + count, row : row + buffer.shape[1], :],
            sems.at[sem],
        )

    def place(tile, index, buffer, part):
        for group, lane in enumerate(groups):
            buffer[part, group * share : (group + 1) * share, :] = tile[
                index * share : (index + 1) * share, lane : lane + LANES
            ]

    rows = [own_rows[...]] + residual((far0, far1), cross_far[...], solved[...], white[...], right)
    tile = tile_of(left, right)
    for part in range(parts):
        place(tile, part, far_part, part)
    copies = [sent(far_part, 0, parts, 0, 0)]
    copies[0].start()
    rows += residual((near.at[0], near.at[1]), cross_near[...], solved[...], white[...], right)
    rows = jnp.concatenate(rows + [jnp.zeros((1, width), BF16)], 0)
    rows = jnp.concatenate([rows[:, lane : lane + LANES] for lane in groups], 0)
    half = parts // 2
    for group in range(2):
        tile = tile_of(left.at[:, group * half * share : (group + 1) * half * share], right)
        for index in range(half):
            part = group * half + index
            place(tile, index, near_part, part)
            near_part[part, tall:, :] = rows
        copies.append(sent(near_part, group * half, half, tall, 1 + group))
        copies[-1].start()
    for copy in copies:
        copy.wait()


def factored(sums, covariates, padded):
    count, samples = covariates[0].shape
    return pl.pallas_call(
        functools.partial(factor_kernel, count + 1),
        out_shape=(
            jax.ShapeDtypeStruct((padded, padded), F32),
            jax.ShapeDtypeStruct((6 * padded, 2 * samples), BF16),
        ),
        scratch_shapes=[pltpu.VMEM((padded, 2 * samples), F32)],
        compiler_params=pltpu.CompilerParams(vmem_limit_bytes=4 << 20),
        cost_estimate=pl.CostEstimate(flops=3_000_000_000, bytes_accessed=10_000_000, transcendentals=0),
        name="factored",
    )(sums, *covariates)


def own_residual(own, cross, solved, white):
    samples, width = own[0].shape
    return pl.pallas_call(
        own_kernel,
        out_shape=(
            jax.ShapeDtypeStruct((2 * samples, width), BF16),
            jax.ShapeDtypeStruct((1, width), BF16),
        ),
        compiler_params=pltpu.CompilerParams(vmem_limit_bytes=8 << 20),
        cost_estimate=pl.CostEstimate(flops=800_000_000, bytes_accessed=4_000_000, transcendentals=0),
        name="own_residual",
    )(*own, cross, solved, white)


def tiles(far, near, cross_far, cross_near, solved, white, left, own_rows, parts):
    samples, width = far[0].shape
    share = width // parts
    tall = share * width // LANES
    extra = 4 * width // LANES
    return pl.pallas_call(
        tiles_kernel,
        out_shape=jax.ShapeDtypeStruct((parts, 2 * tall + extra, LANES), BF16),
        out_specs=pl.BlockSpec(memory_space=pl.ANY),
        scratch_shapes=[
            pltpu.VMEM((2 * samples, width), BF16),
            pltpu.VMEM((parts, tall, LANES), BF16),
            pltpu.VMEM((parts, tall + extra, LANES), BF16),
            pltpu.SemaphoreType.DMA((3,)),
        ],
        compiler_params=pltpu.CompilerParams(vmem_limit_bytes=16 << 20),
        cost_estimate=pl.CostEstimate(flops=2_000_000_000, bytes_accessed=6_000_000, transcendentals=0),
        name="tiles",
    )(*far, near, cross_far, cross_near, solved, white, left, own_rows)


def bands_kernel(samples, marks_ref, arrived_ref, out_ref):
    parts = arrived_ref.shape[0]
    share, width = out_ref.shape[1:]
    groups = width // LANES
    tall = share * groups

    def wide(rows, height):
        return jnp.concatenate([rows[g * height : (g + 1) * height] for g in range(groups)], 1)

    far, near, weights = [], [], []
    for side in range(2):
        whole = sum(arrived_ref[part].astype(F32) for part in range(side, parts, 2))
        far.append(wide(whole[:tall], share))
        near.append(wide(whole[tall : 2 * tall], share))
        spread = wide(whole[2 * tall :], 4)
        weights.append([jnp.sqrt(samples / spread[at : at + 1]) for at in range(3)])
    row = lax.broadcasted_iota(jnp.int32, (share, width), 0)
    mine = row == marks_ref[0:1, :]
    reached = marks_ref[1:2, :]
    own = jnp.sum(jnp.where(mine, weights[0][0], 0.0), 1, keepdims=True) * (1.0 / math.sqrt(samples))
    slots = [
        (far[1], weights[1][1], 2),
        (near[1], weights[1][2], 1),
        (near[0], weights[0][2], 1),
        (far[0], weights[0][1], 2),
    ]
    for slot, (total, weight, offset) in enumerate(slots):
        live = reached >= offset
        out_ref[slot] = jnp.where(live, total * own * weight, 0.0).astype(BF16)


def bands(place, reached, arrived, samples, width):
    share = width // arrived.shape[0]
    vmem = pl.BlockSpec(memory_space=pltpu.VMEM)
    lanes = jnp.arange(width, dtype=jnp.int32) - place * share
    marks = jnp.stack([lanes, jnp.full((width,), reached, jnp.int32)])
    return pl.pallas_call(
        functools.partial(bands_kernel, samples),
        out_shape=jax.ShapeDtypeStruct((2 * MAXR, share, width), BF16),
        in_specs=[vmem, vmem],
        out_specs=vmem,
        compiler_params=pltpu.CompilerParams(vmem_limit_bytes=8 << 20),
        name="bands",
    )(marks, arrived)


def exchange(x):
    return lax.all_to_all(x, "sample", 0, 0, tiled=False)


def shards(dosage, covariates, reach):
    local_samples, width = dosage.shape
    parts = lax.axis_size("sample")
    blocks = lax.axis_size("variant")
    half = parts // 2
    samples = local_samples * parts
    place = lax.axis_index("sample")
    core = lax.axis_index("variant") % 2
    side = place % 2
    padded = -(-(covariates.shape[0] + 1) // parts) * parts
    both = ("sample", "variant")

    partner_route = [(i, i ^ 1) for i in range(parts)]
    core_route = [(i, i ^ 1) for i in range(blocks)]
    far_route = []
    near_route = []
    for s in range(parts):
        step = MAXR if s % 2 == 0 else -MAXR
        for v in range(blocks):
            far_route.append((s * blocks + (v + step) % blocks, s * blocks + v))
            near_route.append((s * blocks + (v + step // MAXR) % blocks, s * blocks + v))

    def from_partner(x):
        return lax.ppermute(x, "sample", partner_route)

    def from_far(x):
        return lax.ppermute(x, both, far_route)

    def for_mate(own, far):
        return jnp.where(core != side, own, far)

    def swap(x):
        return lax.ppermute(x, "variant", core_route)

    def after(x, *earlier):
        return lax.optimization_barrier((x,) + earlier)[0]

    own0 = dosage
    covariates1 = from_partner(covariates)
    message = local_sums(dosage, covariates, padded, parts)
    sent = own0
    own1 = from_partner(sent)
    far0 = from_far(sent)
    sums = exchange(message)
    chunk = sums[:, :, :width].sum(0)
    message = jnp.broadcast_to(chunk[None], (parts,) + chunk.shape)
    message = after(message, own1, far0, covariates1)
    far1 = from_far(after(own1, message))
    cross = exchange(message).reshape(padded, width)
    solved, white = factored(after(sums, message), (covariates, covariates1), padded)
    cross_far = from_far(cross)
    left, own_rows = own_residual((own0, own1), cross, solved, white)
    cross_near = lax.ppermute(cross, both, near_route)
    near = swap(after(for_mate(jnp.stack([own0, own1]), jnp.stack([far0, far1])), left))
    message = tiles(
        (far0, far1), near, cross_far, cross_near, solved, white, left, own_rows, parts
    )
    reached = reach[lax.axis_index("variant")]
    return bands(place, reached, exchange(message), samples, width)


def solution(mesh):
    placed = (P("sample", "variant"), P(None, "sample"), P())
    return jax.shard_map(
        shards,
        mesh=mesh,
        in_specs=placed,
        out_specs=P(None, ("variant", "sample"), None),
        check_vma=False,
    )
```
